32 devices in a mesh: grp: 4 (over x, core), mem: 8 (over z, y).
Axes of the slice: x: 2, y: 2, z: 4, core: 2. Of those that a mesh axis runs over, the one named last changes fastest.
Arguments:
- embeddings: bfloat16 [16384, 768], P(('grp', 'mem')), may hold values from -1500 to 1500
- cluster_id: int32 [16384], P(('grp', 'mem')), may hold values from 0 to 3, as said below
- row_order: int32 [16384], P(('grp', 'mem')), may hold values from 0 to 16383, each once
- assignment: int32 [4], replicated, may hold values from 0 to 3, as said below
- placement: int32 [16384], P(('grp', 'mem')), may hold values from 0 to 7
Outputs:
- owner_best: float32 [32768], P(('grp', 'mem'))
The draws below stay inside these ranges and needn't reach their ends.
Inputs may be any that keep to these rules, and one draw needn't show every extreme that they name: `cluster_id`: owner = assignment * 8 + placement; at most 32 rows of one device share an owner, and in every draw some owner gets exactly 32 rows from every device. `assignment`: each group owns exactly 1 cluster.
All inputs are finite; a program needn't handle non-finite values.
Results may differ from the reference program's by a relative error of at most 0.00034.
Values may be sent and summed in bfloat16 or wider, within the bound.
A program may use at most 128 MiB of HBM per device.

```python
import math
import jax
import jax.numpy as jnp
from jax import lax

D = 768
ROWS_DEV = 512
CL_GRP = 1
GROUPS = 4
MEMBERS = 8
OWNERS = 32
CAP = 32
SLOTS = 1024
ROWS = 16384
CLUSTERS = 4


def route_plan(key):
    base_key = jax.random.fold_in(key, 5)
    key_perm, key_hot, key_dest, key_pick = jax.random.split(base_key, 4)
    shuffled = jax.random.permutation(key_perm, CLUSTERS)
    assignment = shuffled % GROUPS
    listing = jnp.argsort(shuffled)
    hot_owner = jax.random.randint(key_hot, (), 0, OWNERS)
    others = jnp.arange((OWNERS - 1) * CAP) // CAP
    others = others + (others >= hot_owner).astype(others.dtype)

    def per_source(source_key):
        key_take, key_mix = jax.random.split(source_key)
        picked = jax.random.permutation(key_take, (OWNERS - 1) * CAP)[:ROWS_DEV - CAP]
        targets = jnp.concatenate([jnp.full((CAP,), hot_owner, others.dtype), others[picked]])
        return jax.random.permutation(key_mix, targets)
    targets = jax.vmap(per_source)(jax.random.split(key_dest, OWNERS)).reshape(ROWS)
    within = jax.random.randint(key_pick, (ROWS,), 0, CL_GRP)
    cluster_id = listing[targets // MEMBERS + GROUPS * within]
    placement = targets % MEMBERS
    return (cluster_id.astype(jnp.int32), assignment.astype(jnp.int32), placement.astype(jnp.int32))


def draw_cluster_id(key, part):
    return route_plan(key)[0]


def draw_assignment(key, part):
    return route_plan(key)[1]


def draw_placement(key, part):
    return route_plan(key)[2]


def draw_embeddings(key, part):
    cluster_id = route_plan(key)[0]
    key_base, key_shared, key_weight, key_scale = jax.random.split(jax.random.fold_in(key, 11), 4)
    noise = jax.random.truncated_normal(key_base, -4.0, 4.0, (ROWS, D), jnp.float32)
    shared = jax.random.truncated_normal(key_shared, -4.0, 4.0, (ROWS, D), jnp.float32)
    sorter = jnp.argsort(cluster_id, stable=True)
    sorted_ids = cluster_id[sorter]
    position = jnp.arange(ROWS)
    partner = jnp.minimum(position ^ 1, ROWS - 1)
    paired = sorted_ids[partner] == sorted_ids
    anchor_sorted = jnp.where(paired, sorter[jnp.minimum(position, partner)], sorter)
    anchor = jnp.zeros((ROWS,), jnp.int32).at[sorter].set(anchor_sorted.astype(jnp.int32))
    weight = jax.random.uniform(key_weight, (ROWS, 1), jnp.float32, 1.0, 4.0)
    values = noise + weight * shared[anchor]
    row_scale = jnp.exp(jax.random.uniform(key_scale, (ROWS, 1), jnp.float32, 0.0, 2.302585))
    return (values * row_scale).astype(jnp.bfloat16)


def setup_inputs(seed: int = 0) -> dict:
    seeds = jax.random.split(jax.random.key(seed), 6)
    embeddings = draw_embeddings(jax.random.fold_in(seeds[5], 71), 0)
    cluster_id = draw_cluster_id(jax.random.fold_in(seeds[5], 71), 0)
    row_order = jax.random.permutation(seeds[2], ROWS).astype(jnp.int32)
    assignment = draw_assignment(jax.random.fold_in(seeds[5], 71), 0)
    placement = draw_placement(jax.random.fold_in(seeds[5], 71), 0)
    return dict(embeddings=embeddings, cluster_id=cluster_id, row_order=row_order, assignment=assignment, placement=placement)


def reference(embeddings, cluster_id, row_order, assignment, placement):
    widened = embeddings.astype(jnp.float32)
    feature_count = widened.shape[1]
    rounded = (widened * lax.rsqrt(lax.optimization_barrier(jnp.mean(widened * widened, axis=1, keepdims=True)) + 1e-06) * (1.0 / math.sqrt(feature_count))).astype(jnp.bfloat16)
    unit_rows = lax.optimization_barrier(rounded).astype(jnp.float32)
    row_count = unit_rows.shape[0]
    block_rows = 512 if row_count % 512 == 0 else row_count
    blocks = row_count // block_rows

    def block_max(packed):
        block_units, block_cluster, block_order = packed
        scores = jnp.dot(block_units, unit_rows.T, precision=lax.Precision.HIGHEST)
        eligible = (block_cluster[:, None] == cluster_id[None, :]) & (row_order[None, :] < block_order[:, None])
        return jnp.maximum(lax.optimization_barrier(jnp.max(jnp.where(eligible, scores, -2.0), axis=1)), -1.0)
    similar = lax.map(block_max, (unit_rows.reshape(blocks, block_rows, feature_count), cluster_id.reshape(blocks, block_rows), row_order.reshape(blocks, block_rows))).reshape(row_count)
    owner_id = (assignment[cluster_id] * MEMBERS + placement).astype(jnp.int32).reshape(OWNERS, ROWS_DEV)
    owner_hits = (owner_id[:, :, None] == jnp.arange(OWNERS).astype(jnp.int32)[None, None, :]).astype(jnp.int32)
    rank_in_source = lax.optimization_barrier(jnp.sum((jnp.cumsum(owner_hits, axis=1) - 1) * owner_hits, axis=2)).astype(jnp.int32)
    source_id = jnp.arange(OWNERS).astype(jnp.int32)[:, None]
    slot_index = (owner_id * SLOTS + source_id * CAP + rank_in_source).reshape(row_count).astype(jnp.int32)
    return jnp.full((OWNERS * SLOTS,), -1.0, jnp.float32).at[slot_index].set(similar)
```

```python
import functools
import math

import jax
import jax.numpy as jnp
from jax import lax
from jax.experimental import pallas as pl
from jax.experimental.pallas import tpu as pltpu
from jax.sharding import PartitionSpec as P

MESH = pl.DeviceIdType.MESH
NZ = 4
CHUNKS = 4
TILE = 256
LOW = -2.0


def flip(index, mask):
    out, bit = index, 1
    while bit <= mask:
        if mask & bit:
            out = out + bit - 2 * bit * (lax.div(index, bit) % 2)
        bit *= 2
    return out


def kernel(
    groups, ys, units, meta, best, planes, zs, plane_meta, z_meta, col_acc, row_acc,
    row_key, row_cluster, back, z_back, z_send, ready_sem, p_send, p_recv, z_ssem, z_rsem,
    pm_send, pm_recv, zm_send, zm_recv, b_send, b_recv, zb_send, zb_recv, relay_sem,
):
    g, m = lax.axis_index("grp"), lax.axis_index("mem")
    z, y = lax.div(m, ys), m % ys
    tiles = (groups // 2) * ys
    count = 2 * tiles
    rows = planes.shape[1]
    part = rows // CHUNKS

    def plane_peer(d):
        j, c = d // 2, d % 2
        return (flip(g, (j // ys) * 2 + c), z * ys + flip(y, j % ys))

    def column_peer(dz):
        return (g, ((z + dz) % NZ) * ys + y)

    load = pltpu.make_async_copy(units, planes.at[0], ready_sem)
    load.start()

    barrier = pltpu.get_barrier_semaphore()
    peers = [plane_peer(d) for d in range(1, count)] + [column_peer(k) for k in range(1, NZ)]
    for peer in peers:
        pl.semaphore_signal(barrier, inc=1, device_id=peer, device_id_type=MESH)
    col_acc[...] = jnp.full(col_acc.shape, LOW, jnp.float32)
    row_acc[...] = jnp.full(row_acc.shape, LOW, jnp.float32)
    plane_meta[0] = meta[...]
    load.wait()
    pl.semaphore_wait(barrier, len(peers))

    def remote(src, dst, ssem, rsem, peer):
        return pltpu.make_async_remote_copy(
            src_ref=src, dst_ref=dst, send_sem=ssem, recv_sem=rsem,
            device_id=peer, device_id_type=MESH,
        )

    def piece(k):
        return pl.ds(k * part, part)

    def own_to_z(k, slot, dz):
        return remote(
            planes.at[0, piece(k)], zs.at[slot, piece(k)], z_ssem.at[slot, k],
            z_rsem.at[slot, k], column_peer(dz),
        )

    def relay(k, src, dst, dz):
        return remote(
            zs.at[src, piece(k)], zs.at[dst, piece(k)], relay_sem.at[src, k],
            z_rsem.at[dst, k], column_peer(dz),
        )

    def to_plane(d):
        return remote(planes.at[0], planes.at[d], p_send.at[d], p_recv.at[d], plane_peer(d))

    def forward(j):
        return remote(
            planes.at[2 * j], planes.at[2 * j + 1], p_send.at[2 * j + 1], p_recv.at[2 * j + 1],
            plane_peer(1),
        )

    meta_copies = [
        remote(meta, plane_meta.at[d], pm_send.at[d], pm_recv.at[d], plane_peer(d))
        for d in range(1, count)
    ] + [
        remote(meta, z_meta.at[s], zm_send.at[s], zm_recv.at[s], column_peer(-1 - s))
        for s in range(2)
    ]
    for copy in meta_copies:
        copy.start()

    to_plane(1).start()

    @pl.when(z >= 1)
    def _():
        for k in range(CHUNKS):
            own_to_z(k, 0, -1).start()

    @pl.when(z <= 1)
    def _():
        for k in range(CHUNKS):
            own_to_z(k, 1, 2).start()

    for j in range(1, tiles):
        to_plane(2 * j).start()

    def spread(a, source):
        row_key[a] = jnp.broadcast_to(source[0:1, :], (128, rows)).T
        row_cluster[a] = jnp.broadcast_to(source[1:2, :], (128, rows)).T

    def pairs(a, left, d, both):
        right = planes[d]
        keys, clusters = plane_meta[d, 0:1, :], plane_meta[d, 1:2, :]

        def step(i, carry):
            here = pl.ds(pl.multiple_of(i * TILE, TILE), TILE)
            scores = lax.dot_general(
                left[here, :], right, (((1,), (1,)), ((), ())),
                preferred_element_type=jnp.float32,
            )
            my_key, my_cluster = row_key[a, here, :], row_cluster[a, here, :]
            acc = row_acc[a, here, :]
            for t in range(rows // 128):
                lanes = slice(t * 128, (t + 1) * 128)
                kept = jnp.where(my_cluster == clusters[:, lanes], scores[:, lanes], LOW)
                earlier = keys[:, lanes] < my_key
                acc = jnp.maximum(acc, jnp.where(earlier, kept, LOW))
                if both:
                    other = jnp.where(earlier, LOW, kept).reshape(TILE // 8, 8, 128)
                    col_acc[d, :, lanes] = jnp.maximum(col_acc[d, :, lanes], jnp.max(other, axis=0))
            row_acc[a, here, :] = acc
            return carry

        lax.fori_loop(0, rows // TILE, step, 0)

    spread(0, meta)
    own = planes.at[0]
    pairs(0, own, 0, False)
    for copy in meta_copies:
        copy.wait()
    to_plane(1).wait_recv()
    pairs(0, own, 1, False)

    for k in range(CHUNKS):
        @pl.when((z == 1) | (z == 2))
        def _():
            own_to_z(k, 0, -1).wait_recv()
            relay(k, 0, 1, -1).start()

        @pl.when(z == 2)
        def _():
            own_to_z(k, 1, 2).wait_recv()
            relay(k, 1, 0, 1).start()

    def plane_step(j, carry):
        pltpu.make_async_copy(planes.at[2 * j], planes.at[2 * j], p_recv.at[2 * j]).wait()
        forward(j).start()
        pairs(0, own, 2 * j, False)
        forward(j).wait_recv()
        pairs(0, own, 2 * j + 1, False)
        return carry

    lax.fori_loop(1, tiles, plane_step, 0)

    for k in range(CHUNKS):
        @pl.when((z == 0) | (z == 3))
        def _():
            own_to_z(k, 0, -1).wait_recv()

        @pl.when(z != 2)
        def _():
            own_to_z(k, 1, 2).wait_recv()

    spread(1, z_meta.at[0])
    spread(2, z_meta.at[1])

    def z1_step(d, carry):
        pairs(1, zs.at[0], d, True)
        return carry

    lax.fori_loop(0, count, z1_step, 0)
    first = lax.div(z, 2) * (count // 2)

    def z2_step(d, carry):
        pairs(2, zs.at[1], d + first, True)
        return carry

    lax.fori_loop(0, count // 2, z2_step, 0)

    def fold(a):
        return jnp.max(row_acc[a].T.reshape(16, 8, rows), axis=0)

    z_send[0] = fold(1)
    z_send[1] = fold(2)
    result_copies = [
        remote(col_acc.at[d], back.at[d], b_send.at[d], b_recv.at[d], plane_peer(d))
        for d in range(1, count)
    ]
    for copy in result_copies:
        copy.start()
    mine = jnp.maximum(fold(0), col_acc[0])
    z_copies = [
        remote(z_send.at[s], z_back.at[s], zb_send.at[s], zb_recv.at[s], column_peer(1 + s))
        for s in range(2)
    ]
    for copy in z_copies:
        copy.start()

    @pl.when(z >= 1)
    def _():
        for k in range(CHUNKS):
            own_to_z(k, 0, -1).wait_send()

    @pl.when(z <= 1)
    def _():
        for k in range(CHUNKS):
            own_to_z(k, 1, 2).wait_send()

    @pl.when((z == 1) | (z == 2))
    def _():
        for k in range(CHUNKS):
            relay(k, 0, 1, -1).wait_send()

    @pl.when(z == 2)
    def _():
        for k in range(CHUNKS):
            relay(k, 1, 0, 1).wait_send()

    to_plane(1).wait_send()
    for j in range(1, tiles):
        to_plane(2 * j).wait_send()
        forward(j).wait_send()

    for copy in result_copies + z_copies:
        copy.wait()
    for d in range(1, count):
        mine = jnp.maximum(mine, back[d])
    mine = jnp.maximum(mine, jnp.maximum(z_back[0], z_back[1]))
    best[...] = jnp.maximum(jnp.max(mine, axis=0, keepdims=True), -1.0)


def similarities(units, meta, groups, members):
    rows, width = units.shape
    ys = members // NZ
    count = groups * ys
    dma = pltpu.SemaphoreType.DMA
    return pl.pallas_call(
        functools.partial(kernel, groups, ys),
        out_shape=jax.ShapeDtypeStruct((1, rows), jnp.float32),
        in_specs=[
            pl.BlockSpec(memory_space=pl.ANY),
            pl.BlockSpec(memory_space=pltpu.VMEM),
        ],
        out_specs=pl.BlockSpec(memory_space=pltpu.VMEM),
        scratch_shapes=[
            pltpu.VMEM((count, rows, width), jnp.bfloat16),
            pltpu.VMEM((2, rows, width), jnp.bfloat16),
            pltpu.VMEM((count, 2, rows), jnp.float32),
            pltpu.VMEM((2, 2, rows), jnp.float32),
            pltpu.VMEM((count, 8, rows), jnp.float32),
            pltpu.VMEM((3, rows, 128), jnp.float32),
            pltpu.VMEM((3, rows, 128), jnp.float32),
            pltpu.VMEM((3, rows, 128), jnp.float32),
            pltpu.VMEM((count, 8, rows), jnp.float32),
            pltpu.VMEM((2, 8, rows), jnp.float32),
            pltpu.VMEM((2, 8, rows), jnp.float32),
            dma(()),
            dma((count,)), dma((count,)),
            dma((2, CHUNKS)), dma((2, CHUNKS)),
            dma((count,)), dma((count,)),
            dma((2,)), dma((2,)),
            dma((count,)), dma((count,)),
            dma((2,)), dma((2,)),
            dma((2, CHUNKS)),
        ],
        compiler_params=pltpu.CompilerParams(
            collective_id=0, has_side_effects=True, vmem_limit_bytes=56 * 1024 * 1024
        ),
    )(units, meta)


def local(embeddings, cluster_id, row_order, assignment, placement):
    members = lax.axis_size("mem")
    groups = lax.axis_size("grp")
    owners = groups * members
    row_count, feature_count = embeddings.shape
    capacity = max(2, 2 * row_count // owners)
    widened = embeddings.astype(jnp.float32)
    unit_rows = (
        widened
        * lax.rsqrt(jnp.mean(widened * widened, axis=1, keepdims=True) + 1e-06)
        * (1.0 / math.sqrt(feature_count))
    ).astype(jnp.bfloat16)
    meta = jnp.stack([row_order, cluster_id]).astype(jnp.float32)
    best = similarities(unit_rows, meta, groups, members)

    table_hits = cluster_id[:, None] == jnp.arange(assignment.shape[0], dtype=jnp.int32)[None, :]
    group_of = jnp.sum(jnp.where(table_hits, assignment[None, :], 0), axis=1)
    owner_id = group_of * members + placement
    before = jnp.arange(row_count)[None, :] < jnp.arange(row_count)[:, None]
    rank = jnp.sum((before & (owner_id[None, :] == owner_id[:, None])).astype(jnp.int32), axis=1)
    target = owner_id * capacity + rank
    slots = jnp.arange(owners * capacity, dtype=jnp.int32)
    filled = jnp.max(
        jnp.where(slots[:, None] == target[None, :], best, -1.0), axis=1
    )
    return lax.all_to_all(filled, ("grp", "mem"), split_axis=0, concat_axis=0, tiled=True)


def solution(mesh):
    return jax.shard_map(
        local,
        mesh=mesh,
        in_specs=(
            P(("grp", "mem"), None),
            P(("grp", "mem")),
            P(("grp", "mem")),
            P(),
            P(("grp", "mem")),
        ),
        out_specs=P(("grp", "mem")),
        check_vma=False,
    )
```

```python
import functools
import math

import jax
import jax.numpy as jnp
from jax import lax
from jax.experimental import pallas as pl
from jax.experimental.pallas import tpu as pltpu
from jax.sharding import PartitionSpec as P

MESH = pl.DeviceIdType.MESH
NZ = 4
CHUNKS = 8
LOW = -2.0


def flip(index, mask):
    out, bit = index, 1
    while bit <= mask:
        if mask & bit:
            out = out + bit - 2 * bit * (lax.div(index, bit) % 2)
        bit *= 2
    return out


def kernel(
    groups, members, rows_in, meta, target, out, planes, zs, plane_meta, z_meta, col_acc,
    row_acc, row_key, row_cluster, back, z_back, z_send, slot_send, slot_recv, p_send, p_recv,
    h_send, h_recv, z_ssem, z_rsem, pm_send, pm_recv, zm_send, zm_recv, b_send, b_recv,
    zb_send, zb_recv, relay_sem, s_send, s_recv,
):
    ys = members // NZ
    g, m = lax.axis_index("grp"), lax.axis_index("mem")
    z, y = lax.div(m, ys), m % ys
    me = g * members + m
    owners = groups * members
    tiles = (groups // 2) * ys
    count = 2 * tiles
    half = count // 2
    rows, width = planes.shape[1], planes.shape[2]
    part = rows // CHUNKS
    square = tiles == 4 and ys == 2
    capacity = out.shape[1]
    shared = 128 // capacity

    def plane_peer(d):
        j, c = d // 2, d % 2
        return (flip(g, (j // ys) * 2 + c), z * ys + flip(y, j % ys))

    def column_peer(dz):
        return (g, ((z + dz) % NZ) * ys + y)

    def other_device(r):
        o = (me + r) % owners
        return o, (lax.div(o, members), o % members)

    barrier = pltpu.get_barrier_semaphore()

    def greet(r, carry):
        pl.semaphore_signal(
            barrier, inc=1, device_id=other_device(r)[1], device_id_type=MESH
        )
        return carry

    lax.fori_loop(1, owners, greet, 0)

    def normalise(i, carry):
        here = pl.ds(pl.multiple_of(i * 64, 64), 64)
        wide = rows_in[here, :].astype(jnp.float32)
        mean = jnp.sum(wide * wide, axis=1, keepdims=True) * (1.0 / width)
        scaled = wide * lax.rsqrt(mean + 1e-06) * (1.0 / math.sqrt(width))
        planes[0, here, :] = scaled.astype(jnp.bfloat16)
        return carry

    lax.fori_loop(0, rows // 64, normalise, 0)
    col_acc[...] = jnp.full(col_acc.shape, LOW, jnp.float32)
    row_acc[...] = jnp.full(row_acc.shape, LOW, jnp.float32)
    plane_meta[0] = meta[...]

    def spread(a, source):
        row_key[a] = jnp.broadcast_to(source[0:1, :], (128, rows)).T
        row_cluster[a] = jnp.broadcast_to(source[1:2, :], (128, rows)).T

    spread(0, meta)
    pl.semaphore_wait(barrier, owners - 1)

    def remote(src, dst, ssem, rsem, peer):
        return pltpu.make_async_remote_copy(
            src_ref=src, dst_ref=dst, send_sem=ssem, recv_sem=rsem,
            device_id=peer, device_id_type=MESH,
        )

    def piece(k):
        return pl.ds(k * part, part)

    def own_to_z(k, slot, dz):
        return remote(
            planes.at[0, piece(k)], zs.at[slot, piece(k)], z_ssem.at[slot, k],
            z_rsem.at[slot, k], column_peer(dz),
        )

    def relay(k, src, dst, dz):
        return remote(
            zs.at[src, piece(k)], zs.at[dst, piece(k)], relay_sem.at[src, k],
            z_rsem.at[dst, k], column_peer(dz),
        )

    def to_plane(d):
        return remote(planes.at[0], planes.at[d], p_send.at[d], p_recv.at[d], plane_peer(d))

    def diagonal(h):
        src, peer = ((2, 4), (4, 2))[h]
        rows_h = pl.ds(h * (rows // 2), rows // 2)
        return remote(
            planes.at[src, rows_h], planes.at[6, rows_h], h_send.at[h], h_recv.at[h],
            plane_peer(peer),
        )

    def forward(j):
        return remote(
            planes.at[2 * j], planes.at[2 * j + 1], p_send.at[2 * j + 1], p_recv.at[2 * j + 1],
            plane_peer(1),
        )

    meta_copies = [
        remote(meta, plane_meta.at[d], pm_send.at[d], pm_recv.at[d], plane_peer(d))
        for d in range(1, count)
    ] + [
        remote(meta, z_meta.at[s], zm_send.at[s], zm_recv.at[s], column_peer(-1 - s))
        for s in range(2)
    ]
    for copy in meta_copies:
        copy.start()

    @pl.when(z >= 1)
    def _():
        for k in range(CHUNKS):
            own_to_z(k, 0, -1).start()

    @pl.when(z <= 1)
    def _():
        for k in range(CHUNKS):
            own_to_z(k, 1, 2).start()

    direct = range(1, tiles - 1 if square else tiles)
    for j in direct:
        to_plane(2 * j).start()
    to_plane(1).start()

    def pairs(a, left, d, start, size, both):
        right = planes[d]
        keys, clusters = plane_meta[d, 0:1, :], plane_meta[d, 1:2, :]
        here = pl.ds(start, size)
        scores = lax.dot_general(
            left[here, :], right, (((1,), (1,)), ((), ())),
            preferred_element_type=jnp.float32,
        )
        my_key, my_cluster = row_key[a, here, :], row_cluster[a, here, :]
        acc = row_acc[a, here, :]
        for t in range(rows // 128):
            lanes = slice(t * 128, (t + 1) * 128)
            kept = jnp.where(my_cluster == clusters[:, lanes], scores[:, lanes], LOW)
            earlier = keys[:, lanes] < my_key
            acc = jnp.maximum(acc, jnp.where(earlier, kept, LOW))
            if both:
                other = jnp.where(earlier, LOW, kept).reshape(size // 8, 8, 128)
                col_acc[d, :, lanes] = jnp.maximum(col_acc[d, :, lanes], jnp.max(other, axis=0))
        row_acc[a, here, :] = acc

    own = planes.at[0]

    def own_pairs(d0, d1):
        def step(d, carry):
            pairs(0, own, d, 0, rows // 2, False)
            pairs(0, own, d, rows // 2, rows // 2, False)
            return carry

        lax.fori_loop(d0, d1, step, 0)

    first = lax.div(z, 2) * half

    def z_pairs(d0, d1, start, size):
        def step(d, carry):
            pairs(1, zs.at[0], d, start, size, True)

            @pl.when((d >= first) & (d < first + half))
            def _():
                pairs(2, zs.at[1], d, start, size, True)

            return carry

        lax.fori_loop(d0, d1, step, 0)

    def own_recv(k, slot):
        own_to_z(k, slot, -1).wait_recv()

    def relays_one(ks):
        @pl.when((z == 1) | (z == 2))
        def _():
            for k in ks:
                own_recv(k, 0)
                relay(k, 0, 1, -1).start()

    def arrive(ks):
        for k in ks:
            @pl.when((z == 0) | (z == 3))
            def _():
                own_recv(k, 0)

            own_recv(k, 1)

            @pl.when(z == 2)
            def _():
                relay(k, 1, 0, 1).start()

    quarter = rows // 4
    per = CHUNKS // 4

    def chunk_range(s):
        return range(s * per, (s + 1) * per)

    own_pairs(0, 1)
    for copy in meta_copies:
        copy.wait()
    to_plane(1).wait_recv()
    own_pairs(1, 2)
    spread(1, z_meta.at[0])
    spread(2, z_meta.at[1])

    relays_one(range(0, 2 * per))
    arrive(chunk_range(0))
    z_pairs(0, 2, 0, quarter)
    relays_one(range(2 * per, 4 * per))
    arrive(chunk_range(1))

    def collect(j, carry):
        pltpu.make_async_copy(planes.at[2 * j], planes.at[2 * j], p_recv.at[2 * j]).wait()
        forward(j).start()
        return carry

    def collect_partner(j, carry):
        forward(j).wait_recv()
        return carry

    lax.fori_loop(1, tiles - 1, collect, 0)
    if square:
        diagonal(0).start()
        diagonal(1).start()
    z_pairs(0, 2, quarter, quarter)
    lax.fori_loop(1, tiles - 1, collect_partner, 0)
    own_pairs(2, count - 2)
    z_pairs(2, count - 2, 0, 2 * quarter)
    arrive(chunk_range(2))
    if square:
        diagonal(0).wait_recv()
        diagonal(1).wait_recv()
        forward(tiles - 1).start()
    else:
        collect(tiles - 1, 0)
    z_pairs(0, count - 2, 2 * quarter, quarter)
    forward(tiles - 1).wait_recv()
    own_pairs(count - 2, count)
    z_pairs(count - 2, count, 0, 2 * quarter)
    z_pairs(count - 2, count, 2 * quarter, quarter)
    arrive(chunk_range(3))
    z_pairs(0, count, 3 * quarter, quarter)

    def fold(a):
        return jnp.max(row_acc[a].T.reshape(16, 8, rows), axis=0)

    z_send[0] = fold(1)
    z_send[1] = fold(2)
    result_copies = [
        remote(col_acc.at[d], back.at[d], b_send.at[d], b_recv.at[d], plane_peer(d))
        for d in range(1, count)
    ]
    for copy in result_copies:
        copy.start()
    mine = jnp.maximum(fold(0), col_acc[0])
    z_copies = [
        remote(z_send.at[s], z_back.at[s], zb_send.at[s], zb_recv.at[s], column_peer(1 + s))
        for s in range(2)
    ]
    for copy in z_copies:
        copy.start()
    wanted = jnp.broadcast_to(target[...], (128, rows)).T

    @pl.when(z >= 1)
    def _():
        for k in range(CHUNKS):
            own_to_z(k, 0, -1).wait_send()

    @pl.when(z <= 1)
    def _():
        for k in range(CHUNKS):
            own_to_z(k, 1, 2).wait_send()

    @pl.when((z == 1) | (z == 2))
    def _():
        for k in range(CHUNKS):
            relay(k, 0, 1, -1).wait_send()

    @pl.when(z == 2)
    def _():
        for k in range(CHUNKS):
            relay(k, 1, 0, 1).wait_send()

    to_plane(1).wait_send()
    for j in direct:
        to_plane(2 * j).wait_send()
    if square:
        diagonal(0).wait_send()
        diagonal(1).wait_send()
    for j in range(1, tiles):
        forward(j).wait_send()

    for copy in result_copies + z_copies:
        copy.wait()
    for d in range(1, count):
        mine = jnp.maximum(mine, back[d])
    mine = jnp.maximum(mine, jnp.maximum(z_back[0], z_back[1]))
    best = jnp.maximum(jnp.max(mine, axis=0, keepdims=True), -1.0)
    similar = jnp.broadcast_to(best, (128, rows)).T
    lane = lax.broadcasted_iota(jnp.int32, (rows, 128), 1).astype(jnp.float32)
    for t in range(slot_send.shape[0]):
        hit = jnp.where(wanted == lane + float(t * 128), similar, -1.0)
        slot_send[t] = jnp.max(hit, axis=0, keepdims=True)

    def slot_copy(r):
        o, peer = other_device(r)
        return remote(
            slot_send.at[lax.div(o, shared)], slot_recv.at[me], s_send.at[r], s_recv.at[me], peer
        )

    def send_slots(r, carry):
        slot_copy(r).start()
        return carry

    def wait_slots(r, carry):
        slot_copy(r).wait_send()
        source = (me + r) % owners
        pltpu.make_async_copy(
            slot_recv.at[source], slot_recv.at[source], s_recv.at[source]
        ).wait()
        return carry

    lax.fori_loop(1, owners, send_slots, 0)
    slot_recv[me] = slot_send[lax.div(me, shared)]
    lax.fori_loop(1, owners, wait_slots, 0)
    got = slot_recv[...].reshape(owners, 128)
    mine_at = me % shared
    picked = got[:, :capacity]
    for q in range(1, shared):
        picked = jnp.where(mine_at == q, got[:, q * capacity : (q + 1) * capacity], picked)
    out[...] = picked


def similarities(embeddings, meta, target, groups, members, capacity):
    rows, width = embeddings.shape
    ys = members // NZ
    count = groups * ys
    owners = groups * members
    dma = pltpu.SemaphoreType.DMA
    vmem = pl.BlockSpec(memory_space=pltpu.VMEM)
    return pl.pallas_call(
        functools.partial(kernel, groups, members),
        out_shape=jax.ShapeDtypeStruct((owners, capacity), jnp.float32),
        in_specs=[vmem, vmem, vmem],
        out_specs=vmem,
        scratch_shapes=[
            pltpu.VMEM((count, rows, width), jnp.bfloat16),
            pltpu.VMEM((2, rows, width), jnp.bfloat16),
            pltpu.VMEM((count, 2, rows), jnp.float32),
            pltpu.VMEM((2, 2, rows), jnp.float32),
            pltpu.VMEM((count, 8, rows), jnp.float32),
            pltpu.VMEM((3, rows, 128), jnp.float32),
            pltpu.VMEM((3, rows, 128), jnp.float32),
            pltpu.VMEM((3, rows, 128), jnp.float32),
            pltpu.VMEM((count, 8, rows), jnp.float32),
            pltpu.VMEM((2, 8, rows), jnp.float32),
            pltpu.VMEM((2, 8, rows), jnp.float32),
            pltpu.VMEM((owners * capacity // 128, 1, 128), jnp.float32),
            pltpu.VMEM((owners, 1, 128), jnp.float32),
            dma((count,)), dma((count,)),
            dma((2,)), dma((2,)),
            dma((2, CHUNKS)), dma((2, CHUNKS)),
            dma((count,)), dma((count,)),
            dma((2,)), dma((2,)),
            dma((count,)), dma((count,)),
            dma((2,)), dma((2,)),
            dma((2, CHUNKS)),
            dma((owners,)), dma((owners,)),
        ],
        compiler_params=pltpu.CompilerParams(
            collective_id=0, has_side_effects=True, vmem_limit_bytes=56 * 1024 * 1024
        ),
    )(embeddings, meta, target)


def local(embeddings, cluster_id, row_order, assignment, placement):
    members = lax.axis_size("mem")
    groups = lax.axis_size("grp")
    owners = groups * members
    row_count = embeddings.shape[0]
    capacity = max(2, 2 * row_count // owners)
    table_hits = cluster_id[:, None] == jnp.arange(assignment.shape[0], dtype=jnp.int32)[None, :]
    group_of = jnp.sum(jnp.where(table_hits, assignment[None, :], 0), axis=1)
    owner_id = group_of * members + placement
    before = jnp.arange(row_count)[None, :] < jnp.arange(row_count)[:, None]
    rank = jnp.sum((before & (owner_id[None, :] == owner_id[:, None])).astype(jnp.int32), axis=1)
    target = (owner_id * capacity + rank).astype(jnp.float32)[None, :]
    meta = jnp.stack([row_order, cluster_id]).astype(jnp.float32)
    filled = similarities(embeddings, meta, target, groups, members, capacity)
    return filled.reshape(owners * capacity)


def solution(mesh):
    return jax.shard_map(
        local,
        mesh=mesh,
        in_specs=(
            P(("grp", "mem"), None),
            P(("grp", "mem")),
            P(("grp", "mem")),
            P(),
            P(("grp", "mem")),
        ),
        out_specs=P(("grp", "mem")),
        check_vma=False,
    )
```

```python
import functools
import math

import jax
import jax.numpy as jnp
from jax import lax
from jax.experimental import pallas as pl
from jax.experimental.pallas import tpu as pltpu
from jax.sharding import PartitionSpec as P

MESH = pl.DeviceIdType.MESH
NZ = 4
CHUNKS = 4
TILE = 256
LOW = -2.0


def flip(index, mask):
    out, bit = index, 1
    while bit <= mask:
        if mask & bit:
            out = out + bit - 2 * bit * (lax.div(index, bit) % 2)
        bit *= 2
    return out


def kernel(
    groups, members, units, meta, target, out, planes, zs, plane_meta, z_meta, col_acc, row_acc,
    row_key, row_cluster, back, z_back, z_send, slot_send, slot_recv, ready_sem, p_send, p_recv, z_ssem, z_rsem,
    pm_send, pm_recv, zm_send, zm_recv, b_send, b_recv, zb_send, zb_recv, relay_sem,
    s_send, s_recv,
):
    ys = members // NZ
    g, m = lax.axis_index("grp"), lax.axis_index("mem")
    z, y = lax.div(m, ys), m % ys
    tiles = (groups // 2) * ys
    count = 2 * tiles
    rows = planes.shape[1]
    part = rows // CHUNKS
    me = g * members + m
    owners = groups * members
    capacity = out.shape[1]
    shared = 128 // capacity

    def plane_peer(d):
        j, c = d // 2, d % 2
        return (flip(g, (j // ys) * 2 + c), z * ys + flip(y, j % ys))

    def column_peer(dz):
        return (g, ((z + dz) % NZ) * ys + y)

    load = pltpu.make_async_copy(units, planes.at[0], ready_sem)
    load.start()

    def other_device(r):
        o = (me + r) % owners
        return o, (lax.div(o, members), o % members)

    barrier = pltpu.get_barrier_semaphore()

    def greet(r, carry):
        pl.semaphore_signal(
            barrier, inc=1, device_id=other_device(r)[1], device_id_type=MESH
        )
        return carry

    lax.fori_loop(1, owners, greet, 0)

    col_acc[...] = jnp.full(col_acc.shape, LOW, jnp.float32)
    row_acc[...] = jnp.full(row_acc.shape, LOW, jnp.float32)
    plane_meta[0] = meta[...]
    load.wait()
    pl.semaphore_wait(barrier, owners - 1)

    def remote(src, dst, ssem, rsem, peer):
        return pltpu.make_async_remote_copy(
            src_ref=src, dst_ref=dst, send_sem=ssem, recv_sem=rsem,
            device_id=peer, device_id_type=MESH,
        )

    def piece(k):
        return pl.ds(k * part, part)

    def own_to_z(k, slot, dz):
        return remote(
            planes.at[0, piece(k)], zs.at[slot, piece(k)], z_ssem.at[slot, k],
            z_rsem.at[slot, k], column_peer(dz),
        )

    def relay(k, src, dst, dz):
        return remote(
            zs.at[src, piece(k)], zs.at[dst, piece(k)], relay_sem.at[src, k],
            z_rsem.at[dst, k], column_peer(dz),
        )

    def to_plane(d):
        return remote(planes.at[0], planes.at[d], p_send.at[d], p_recv.at[d], plane_peer(d))

    def forward(j):
        return remote(
            planes.at[2 * j], planes.at[2 * j + 1], p_send.at[2 * j + 1], p_recv.at[2 * j + 1],
            plane_peer(1),
        )

    meta_copies = [
        remote(meta, plane_meta.at[d], pm_send.at[d], pm_recv.at[d], plane_peer(d))
        for d in range(1, count)
    ] + [
        remote(meta, z_meta.at[s], zm_send.at[s], zm_recv.at[s], column_peer(-1 - s))
        for s in range(2)
    ]
    for copy in meta_copies:
        copy.start()

    to_plane(1).start()

    @pl.when(z >= 1)
    def _():
        for k in range(CHUNKS):
            own_to_z(k, 0, -1).start()

    @pl.when(z <= 1)
    def _():
        for k in range(CHUNKS):
            own_to_z(k, 1, 2).start()

    for j in range(1, tiles):
        to_plane(2 * j).start()

    def spread(a, source):
        row_key[a] = jnp.broadcast_to(source[0:1, :], (128, rows)).T
        row_cluster[a] = jnp.broadcast_to(source[1:2, :], (128, rows)).T

    def pairs(a, left, d, both, t0=0, t1=None):
        right = planes[d]
        keys, clusters = plane_meta[d, 0:1, :], plane_meta[d, 1:2, :]

        def step(i, carry):
            here = pl.ds(pl.multiple_of(i * TILE, TILE), TILE)
            scores = lax.dot_general(
                left[here, :], right, (((1,), (1,)), ((), ())),
                preferred_element_type=jnp.float32,
            )
            my_key, my_cluster = row_key[a, here, :], row_cluster[a, here, :]
            acc = row_acc[a, here, :]
            for t in range(rows // 128):
                lanes = slice(t * 128, (t + 1) * 128)
                kept = jnp.where(my_cluster == clusters[:, lanes], scores[:, lanes], LOW)
                earlier = keys[:, lanes] < my_key
                acc = jnp.maximum(acc, jnp.where(earlier, kept, LOW))
                if both:
                    other = jnp.where(earlier, LOW, kept).reshape(TILE // 8, 8, 128)
                    col_acc[d, :, lanes] = jnp.maximum(col_acc[d, :, lanes], jnp.max(other, axis=0))
            row_acc[a, here, :] = acc
            return carry

        lax.fori_loop(t0, rows // TILE if t1 is None else t1, step, 0)

    spread(0, meta)
    own = planes.at[0]
    pairs(0, own, 0, False)
    for copy in meta_copies:
        copy.wait()
    to_plane(1).wait_recv()
    pairs(0, own, 1, False)

    spread(1, z_meta.at[0])
    spread(2, z_meta.at[1])

    for k in range(CHUNKS):
        @pl.when((z == 1) | (z == 2))
        def _():
            own_to_z(k, 0, -1).wait_recv()
            relay(k, 0, 1, -1).start()

    def pass_on(ks):
        for k in ks:
            @pl.when(z == 2)
            def _():
                own_to_z(k, 1, 2).wait_recv()
                relay(k, 1, 0, 1).start()

    pass_on(range(CHUNKS // 2))

    def plane_step(j, carry):
        pltpu.make_async_copy(planes.at[2 * j], planes.at[2 * j], p_recv.at[2 * j]).wait()
        forward(j).start()
        pairs(0, own, 2 * j, False)
        forward(j).wait_recv()
        pairs(0, own, 2 * j + 1, False)
        return carry

    def arrive(ks):
        for k in ks:
            @pl.when((z == 0) | (z == 3))
            def _():
                own_to_z(k, 0, -1).wait_recv()

            @pl.when(z != 2)
            def _():
                own_to_z(k, 1, 2).wait_recv()

    first = lax.div(z, 2) * (count // 2)
    middle = rows // TILE // 2

    def z_pairs(d0, d1, t0, t1):
        def step(d, carry):
            pairs(1, zs.at[0], d, True, t0, t1)

            @pl.when((d >= first) & (d < first + count // 2))
            def _():
                pairs(2, zs.at[1], d, True, t0, t1)

            return carry

        lax.fori_loop(d0, d1, step, 0)

    lax.fori_loop(1, tiles - 1, plane_step, 0)
    arrive(range(CHUNKS // 2))
    z_pairs(0, count - 2, 0, middle)
    pass_on(range(CHUNKS // 2, CHUNKS))
    plane_step(tiles - 1, 0)
    z_pairs(count - 2, count, 0, middle)
    arrive(range(CHUNKS // 2, CHUNKS))
    z_pairs(0, count, middle, 2 * middle)

    def fold(a):
        return jnp.max(row_acc[a].T.reshape(16, 8, rows), axis=0)

    z_send[0] = fold(1)
    z_send[1] = fold(2)
    result_copies = [
        remote(col_acc.at[d], back.at[d], b_send.at[d], b_recv.at[d], plane_peer(d))
        for d in range(1, count)
    ]
    for copy in result_copies:
        copy.start()
    mine = jnp.maximum(fold(0), col_acc[0])
    z_copies = [
        remote(z_send.at[s], z_back.at[s], zb_send.at[s], zb_recv.at[s], column_peer(1 + s))
        for s in range(2)
    ]
    for copy in z_copies:
        copy.start()

    wanted = jnp.broadcast_to(target[...], (128, rows)).T

    @pl.when(z >= 1)
    def _():
        for k in range(CHUNKS):
            own_to_z(k, 0, -1).wait_send()

    @pl.when(z <= 1)
    def _():
        for k in range(CHUNKS):
            own_to_z(k, 1, 2).wait_send()

    @pl.when((z == 1) | (z == 2))
    def _():
        for k in range(CHUNKS):
            relay(k, 0, 1, -1).wait_send()

    @pl.when(z == 2)
    def _():
        for k in range(CHUNKS):
            relay(k, 1, 0, 1).wait_send()

    to_plane(1).wait_send()
    for j in range(1, tiles):
        to_plane(2 * j).wait_send()
        forward(j).wait_send()

    for copy in result_copies + z_copies:
        copy.wait()
    for d in range(1, count):
        mine = jnp.maximum(mine, back[d])
    mine = jnp.maximum(mine, jnp.maximum(z_back[0], z_back[1]))
    best = jnp.maximum(jnp.max(mine, axis=0, keepdims=True), -1.0)
    similar = jnp.broadcast_to(best, (128, rows)).T
    lane = lax.broadcasted_iota(jnp.int32, (rows, 128), 1).astype(jnp.float32)
    for t in range(slot_send.shape[0]):
        hit = jnp.where(wanted == lane + float(t * 128), similar, -1.0)
        slot_send[t] = jnp.max(hit, axis=0, keepdims=True)

    def slot_copy(r):
        o, peer = other_device(r)
        return remote(
            slot_send.at[lax.div(o, shared)], slot_recv.at[me], s_send.at[r], s_recv.at[me], peer
        )

    def send_slots(r, carry):
        slot_copy(r).start()
        return carry

    def wait_slots(r, carry):
        slot_copy(r).wait_send()
        source = (me + r) % owners
        pltpu.make_async_copy(
            slot_recv.at[source], slot_recv.at[source], s_recv.at[source]
        ).wait()
        return carry

    lax.fori_loop(1, owners, send_slots, 0)
    slot_recv[me] = slot_send[lax.div(me, shared)]
    lax.fori_loop(1, owners, wait_slots, 0)
    got = slot_recv[...].reshape(owners, 128)
    mine_at = me % shared
    picked = got[:, :capacity]
    for q in range(1, shared):
        picked = jnp.where(mine_at == q, got[:, q * capacity : (q + 1) * capacity], picked)
    out[...] = picked


def similarities(units, meta, target, groups, members, capacity):
    rows, width = units.shape
    ys = members // NZ
    count = groups * ys
    owners = groups * members
    dma = pltpu.SemaphoreType.DMA
    return pl.pallas_call(
        functools.partial(kernel, groups, members),
        out_shape=jax.ShapeDtypeStruct((owners, capacity), jnp.float32),
        in_specs=[
            pl.BlockSpec(memory_space=pl.ANY),
            pl.BlockSpec(memory_space=pltpu.VMEM),
            pl.BlockSpec(memory_space=pltpu.VMEM),
        ],
        out_specs=pl.BlockSpec(memory_space=pltpu.VMEM),
        scratch_shapes=[
            pltpu.VMEM((count, rows, width), jnp.bfloat16),
            pltpu.VMEM((2, rows, width), jnp.bfloat16),
            pltpu.VMEM((count, 2, rows), jnp.float32),
            pltpu.VMEM((2, 2, rows), jnp.float32),
            pltpu.VMEM((count, 8, rows), jnp.float32),
            pltpu.VMEM((3, rows, 128), jnp.float32),
            pltpu.VMEM((3, rows, 128), jnp.float32),
            pltpu.VMEM((3, rows, 128), jnp.float32),
            pltpu.VMEM((count, 8, rows), jnp.float32),
            pltpu.VMEM((2, 8, rows), jnp.float32),
            pltpu.VMEM((2, 8, rows), jnp.float32),
            pltpu.VMEM((owners * capacity // 128, 1, 128), jnp.float32),
            pltpu.VMEM((owners, 1, 128), jnp.float32),
            dma(()),
            dma((count,)), dma((count,)),
            dma((2, CHUNKS)), dma((2, CHUNKS)),
            dma((count,)), dma((count,)),
            dma((2,)), dma((2,)),
            dma((count,)), dma((count,)),
            dma((2,)), dma((2,)),
            dma((2, CHUNKS)),
            dma((owners,)), dma((owners,)),
        ],
        compiler_params=pltpu.CompilerParams(
            collective_id=0, has_side_effects=True, vmem_limit_bytes=56 * 1024 * 1024
        ),
    )(units, meta, target)


def local(embeddings, cluster_id, row_order, assignment, placement):
    members = lax.axis_size("mem")
    groups = lax.axis_size("grp")
    owners = groups * members
    row_count, feature_count = embeddings.shape
    capacity = max(2, 2 * row_count // owners)
    widened = embeddings.astype(jnp.float32)
    unit_rows = (
        widened
        * lax.rsqrt(jnp.mean(widened * widened, axis=1, keepdims=True) + 1e-06)
        * (1.0 / math.sqrt(feature_count))
    ).astype(jnp.bfloat16)
    meta = jnp.stack([row_order, cluster_id]).astype(jnp.float32)

    table_hits = cluster_id[:, None] == jnp.arange(assignment.shape[0], dtype=jnp.int32)[None, :]
    group_of = jnp.sum(jnp.where(table_hits, assignment[None, :], 0), axis=1)
    owner_id = group_of * members + placement
    before = jnp.arange(row_count)[None, :] < jnp.arange(row_count)[:, None]
    rank = jnp.sum((before & (owner_id[None, :] == owner_id[:, None])).astype(jnp.int32), axis=1)
    target = (owner_id * capacity + rank).astype(jnp.float32)[None, :]
    filled = similarities(unit_rows, meta, target, groups, members, capacity)
    return filled.reshape(owners * capacity)


def solution(mesh):
    return jax.shard_map(
        local,
        mesh=mesh,
        in_specs=(
            P(("grp", "mem"), None),
            P(("grp", "mem")),
            P(("grp", "mem")),
            P(),
            P(("grp", "mem")),
        ),
        out_specs=P(("grp", "mem")),
        check_vma=False,
    )
```
